32 devices in a mesh: dp: 8 (over z, y), mp: 4 (over x, core).
Axes of the slice: x: 2, y: 2, z: 4, core: 2. Of those that a mesh axis runs over, the one named last changes fastest.
Arguments:
- tokens: bfloat16 [14592, 768], P(('dp', 'mp')), may hold values from -6 to 6
- caption_mask: int32 [64, 128], P('dp'), may hold values from 0 to 1, as said below
- region_counts: int32 [16], replicated, may hold values from 36 to 100, as said below
- group_ids: int32 [64], P('dp'), may hold values from 0 to 15, as said below
- query_weight: bfloat16 [768, 768], P(None, 'mp'), may hold values from -0.21875 to 0.21875
- query_bias: float32 [768], P('mp'), may hold values from -3 to 3
- key_weight: bfloat16 [768, 768], P(None, 'mp'), may hold values from -0.21875 to 0.21875
- value_weight: bfloat16 [768, 768], P(None, 'mp'), may hold values from -0.21875 to 0.21875
- value_bias: float32 [768], P('mp'), may hold values from -3 to 3
- out_weight: bfloat16 [768, 768], P('mp'), may hold values from -1.25 to 1.25
- out_bias: float32 [768], replicated, may hold values from -3 to 3
- attn_gain: float32 [768], replicated, may hold values from 0.5 to 1.5
- attn_shift: float32 [768], replicated, may hold values from -3 to 3
- up_weight: bfloat16 [768, 3072], P(None, 'mp'), may hold values from -0.21875 to 0.21875
- up_bias: float32 [3072], P('mp'), may hold values from -3 to 3
- down_weight: bfloat16 [3072, 768], P('mp'), may hold values from -0.109375 to 0.109375
- down_bias: float32 [768], replicated, may hold values from -3 to 3
- final_gain: float32 [768], replicated, may hold values from 0.5 to 1.5
- final_shift: float32 [768], replicated, may hold values from -3 to 3
- cotangent: bfloat16 [14592, 768], P(('dp', 'mp')), may hold values from -6 to 6
Outputs:
- layer_out: bfloat16 [14592, 768], P(('dp', 'mp'))
- grad_tokens: float32 [14592, 768], P(('dp', 'mp'))
- grad_query_weight: float32 [768, 768], P(None, 'mp')
- grad_query_bias: float32 [768], P('mp')
- grad_key_weight: float32 [768, 768], P(None, 'mp')
- grad_value_weight: float32 [768, 768], P(None, 'mp')
- grad_value_bias: float32 [768], P('mp')
- grad_out_weight: float32 [768, 768], P('mp')
- grad_out_bias: float32 [768], replicated
- grad_attn_gain: float32 [768], replicated
- grad_attn_shift: float32 [768], replicated
- grad_up_weight: float32 [768, 3072], P(None, 'mp')
- grad_up_bias: float32 [3072], P('mp')
- grad_down_weight: float32 [3072, 768], P('mp')
- grad_down_bias: float32 [768], replicated
- grad_final_gain: float32 [768], replicated
- grad_final_shift: float32 [768], replicated
The draws below stay inside these ranges and needn't reach their ends.
Inputs may be any that keep to these rules, and one draw needn't show every extreme that they name: `caption_mask`: each row is ones followed by zeros, with at least one one; some row is all ones. `region_counts`: some image has exactly 100 regions. `group_ids`: each image is named by exactly 4 sequences.
All inputs are finite; a program needn't handle non-finite values.
Results may differ from the reference program's by a relative error of at most 0.015.
Values may be sent and summed in bfloat16 or wider, within the bound.
A program may use at most 128 MiB of HBM per device.

```python
import jax
import jax.numpy as jnp
from jax import lax

D = 768
HEADS = 12
HEAD = 64
FF = 3072
CAP = 128
MAXREG = 100
MINREG = 36
SEQ_DEV = 8
LEN = 228
SEQS = 64
IMAGES = 16
TOKENS = 14592


def draw_caption_mask(key, part):
    first, second = jax.random.split(key)
    lengths = jax.random.randint(first, (SEQS,), 1, CAP + 1)
    full_row = jax.random.randint(second, (), 0, SEQS)
    lengths = lengths.at[full_row].set(CAP)
    slots = jnp.arange(CAP, dtype=jnp.int32)
    return (slots[None, :] < lengths[:, None]).astype(jnp.int32)


def draw_region_counts(key, part):
    first, second = jax.random.split(key)
    counts = jax.random.randint(first, (IMAGES,), MINREG, MAXREG + 1)
    largest = jax.random.randint(second, (), 0, IMAGES)
    return counts.at[largest].set(MAXREG).astype(jnp.int32)


def draw_group_ids(key, part):
    order = jax.random.permutation(key, SEQS)
    return (order % IMAGES).astype(jnp.int32)


def level_of(key, extent, cuts, smallest, high):
    def one(axis_at, blocks):
        heights = jax.random.uniform(jax.random.fold_in(jax.random.fold_in(key, 6), axis_at), (blocks,), jnp.float32, smallest / len(cuts), high / len(cuts))
        return jnp.repeat(jnp.exp(heights), extent[axis_at] // blocks).reshape((-1,) + (1,) * (len(extent) - axis_at - 1))

    level = one(*cuts[0])
    for cut in cuts[1:]:
        level = level * one(*cut)
    return level


def centred(own_key, extent, deviation, limit, shards=(), kind=jnp.bfloat16):
    entries = deviation * jax.random.normal(own_key, extent, jnp.float32)
    if shards:
        entries = entries * level_of(own_key, extent, shards, -0.22, 0.18)
    return jnp.clip(entries, -limit, limit).astype(kind)


def setup_inputs(seed: int = 0) -> dict:
    seeds = jax.random.split(jax.random.key(seed), 21)
    return {
        "tokens": centred(seeds[0], (TOKENS, D), 1.0, 6.0, ((0, 32),)),
        "caption_mask": draw_caption_mask(jax.random.fold_in(seeds[20], 71), 0),
        "region_counts": draw_region_counts(jax.random.fold_in(seeds[20], 71), 0),
        "group_ids": draw_group_ids(jax.random.fold_in(seeds[20], 71), 0),
        "query_weight": centred(seeds[4], (D, D), D ** -0.5, 0.21875, ((1, 4),)),
        "query_bias": centred(seeds[5], (D,), 0.5, 3.0, ((0, 4),), jnp.float32),
        "key_weight": centred(seeds[6], (D, D), D ** -0.5, 0.21875, ((1, 4),)),
        "value_weight": centred(seeds[7], (D, D), D ** -0.5, 0.21875, ((1, 4),)),
        "value_bias": centred(seeds[8], (D,), 0.5, 3.0, ((0, 4),), jnp.float32),
        "out_weight": centred(seeds[9], (D, D), (D // 32) ** -0.5, 1.25, ((0, 4),)),
        "out_bias": centred(seeds[10], (D,), 0.5, 3.0, (), jnp.float32),
        "attn_gain": jnp.clip(1.0 + 0.1 * jax.random.normal(seeds[11], (D,), jnp.float32), 0.5, 1.5),
        "attn_shift": centred(seeds[12], (D,), 0.5, 3.0, (), jnp.float32),
        "up_weight": centred(seeds[13], (D, FF), D ** -0.5, 0.21875, ((1, 4),)),
        "up_bias": centred(seeds[14], (FF,), 0.5, 3.0, ((0, 4),), jnp.float32),
        "down_weight": centred(seeds[15], (FF, D), FF ** -0.5, 0.109375, ((0, 4),)),
        "down_bias": centred(seeds[16], (D,), 0.5, 3.0, (), jnp.float32),
        "final_gain": jnp.clip(1.0 + 0.1 * jax.random.normal(seeds[17], (D,), jnp.float32), 0.5, 1.5),
        "final_shift": centred(seeds[18], (D,), 0.5, 3.0, (), jnp.float32),
        "cotangent": centred(seeds[19], (TOKENS, D), 1.0, 6.0, ((0, 32),)),
    }


EPS = 1e-12
HIGH = lax.Precision.HIGHEST

@jax.custom_vjp
def low(v):
    return lax.optimization_barrier(v.astype(jnp.bfloat16)).astype(jnp.float32)

@jax.custom_vjp
def low_back(v):
    return v

def low_keep(v):
    return (low(v), None)

def low_pass(kept, grad):
    return (grad,)

def back_keep(v):
    return (v, None)

def back_low(kept, grad):
    return (low(grad),)
low.defvjp(low_keep, low_pass)
low_back.defvjp(back_keep, back_low)

def key_valid(caption_mask, region_counts, group_ids):
    images = region_counts.shape[0]
    match = group_ids[:, None] == jnp.arange(images, dtype=jnp.int32)[None, :]
    regions = lax.optimization_barrier(jnp.sum(jnp.where(match, region_counts[None, :], 0), axis=1))
    slots = jnp.arange(MAXREG, dtype=jnp.int32)
    return jnp.concatenate([caption_mask > 0, slots[None, :] < regions[:, None]], axis=1)

def mult(left, right):
    return jnp.dot(left, right, precision=HIGH)

def normalize(total, gain, shift):
    mean = lax.optimization_barrier(jnp.mean(total, axis=-1, keepdims=True))
    centered = total - mean
    spread = lax.optimization_barrier(jnp.mean(centered * centered, axis=-1, keepdims=True))
    return centered * lax.rsqrt(spread + EPS) * gain + shift

def gelu(value):
    return 0.5 * value * (1.0 + jax.scipy.special.erf(value * 0.7071067811865476))

def attend_block(inputs):
    query, keys, values, valid = inputs
    seqs = query.shape[0]
    query_heads = query.reshape(seqs, LEN, HEADS, HEAD)
    key_heads = keys.reshape(seqs, LEN, HEADS, HEAD)
    value_heads = values.reshape(seqs, LEN, HEADS, HEAD)
    scores = low_back(jnp.einsum('sqhd,skhd->shqk', query_heads, key_heads, precision=HIGH) * HEAD ** (-0.5))
    scores = jnp.where(valid[:, None, None, :], scores, -1e+30)
    probs = jax.nn.softmax(scores, axis=-1)
    context = jnp.einsum('shqk,skhd->sqhd', low(probs), value_heads, precision=HIGH)
    return context.reshape(seqs, LEN, D)

def layer(tokens, valid, query_weight, query_bias, key_weight, value_weight, value_bias, out_weight, out_bias, attn_gain, attn_shift, up_weight, up_bias, down_weight, down_bias, final_gain, final_shift):
    query = low(low_back(mult(tokens, query_weight) + query_bias))
    keys = low(low_back(mult(tokens, key_weight)))
    values = low(low_back(mult(tokens, value_weight) + value_bias))
    blocks = SEQS // SEQ_DEV
    shape = (blocks, SEQ_DEV, LEN, D)
    context = lax.map(jax.checkpoint(attend_block), (query.reshape(shape), keys.reshape(shape), values.reshape(shape), valid.reshape(blocks, SEQ_DEV, LEN)))
    context = low(low_back(context.reshape(SEQS * LEN, D)))
    branch = low_back(mult(context, out_weight) + out_bias)
    normed = normalize(tokens + branch, attn_gain, attn_shift)
    act_in = low_back(mult(low(normed), up_weight) + up_bias)
    act = low(gelu(act_in))
    second = low_back(mult(act, down_weight) + down_bias)
    return normalize(normed + second, final_gain, final_shift)

def reference(tokens, caption_mask, region_counts, group_ids, query_weight, query_bias, key_weight, value_weight, value_bias, out_weight, out_bias, attn_gain, attn_shift, up_weight, up_bias, down_weight, down_bias, final_gain, final_shift, cotangent):
    valid = key_valid(caption_mask, region_counts, group_ids)
    weights = tuple((item.astype(jnp.float32) for item in (query_weight, query_bias, key_weight, value_weight, value_bias, out_weight, out_bias, attn_gain, attn_shift, up_weight, up_bias, down_weight, down_bias, final_gain, final_shift)))

    def run(inputs, *params):
        return layer(inputs, valid, *params)
    result, pull = jax.vjp(run, tokens.astype(jnp.float32), *weights)
    grads = pull(cotangent.astype(jnp.float32))
    return (result.astype(jnp.bfloat16), grads[0], grads[1], grads[2], grads[3], grads[4], grads[5], grads[6], grads[7], grads[8], grads[9], grads[10], grads[11], grads[12], grads[13], grads[14], grads[15])
```

```python
import functools

import jax
import jax.numpy as jnp
from jax import lax
from jax.experimental import pallas as pl
from jax.experimental.pallas import tpu as pltpu
from jax.sharding import PartitionSpec as P

HEAD = 64
MAXREG = 100
EPS = 1e-12
ROOT_HALF = 0.7071067811865476
DENSITY = 0.3989422804014327
MASKED = -1e30

D = 768
LEN = 228
MESH = pl.DeviceIdType.MESH
F32 = jnp.float32
BF16 = jnp.bfloat16


def flip(index, bit):
    return index + bit - 2 * bit * ((index // bit) % 2)


class Peers:
    def __init__(self, dp_size):
        self.dp = lax.axis_index("dp")
        self.mp = lax.axis_index("mp")
        self.core = {"dp": self.dp, "mp": flip(self.mp, 1)}
        self.across = {"dp": self.dp, "mp": flip(self.mp, 2)}
        self.pair_at = self.dp % 2
        self.pair = {"dp": flip(self.dp, 1), "mp": self.mp}
        self.line_at = (self.dp // 2) % 4
        self.line = []
        self.line_slot = []
        for step in range(1, 4):
            slot = (self.line_at + step) % 4
            self.line_slot.append(slot)
            self.line.append({"dp": self.dp + 2 * (slot - self.line_at), "mp": self.mp})
        self.extra = []
        bit = 8
        while bit < dp_size:
            self.extra.append({"dp": flip(self.dp, bit), "mp": self.mp})
            bit *= 2
        self.cube = [
            self.core,
            self.across,
            self.pair,
            {"dp": flip(self.dp, 2), "mp": self.mp},
            {"dp": flip(self.dp, 4), "mp": self.mp},
        ] + self.extra


def greet(peers):
    barrier = pltpu.get_barrier_semaphore()
    for peer in peers:
        pl.semaphore_signal(barrier, inc=1, device_id=peer, device_id_type=MESH)
    pl.semaphore_wait(barrier, len(peers))


def remote(src, dst, sems, at, peer):
    return pltpu.make_async_remote_copy(
        src_ref=src,
        dst_ref=dst,
        send_sem=sems.at[0, at],
        recv_sem=sems.at[1, at],
        device_id=peer,
        device_id_type=MESH,
    )


HALF = D // 2
GATHER_CUTS = 2
GATHER_ROWS = HALF // GATHER_CUTS


class Gather:
    def __init__(self, peers, whole, sems):
        self.peers, self.whole, self.sems = peers, whole, sems
        self.own = peers.mp
        self.far = flip(peers.mp, 2)

    def rows(self, half, cut):
        return pl.ds(pl.multiple_of(half * HALF + cut * GATHER_ROWS, GATHER_ROWS), GATHER_ROWS)

    def piece(self, shard, half, cut, at, peer):
        view = self.whole.at[shard, self.rows(half, cut), :]
        return remote(view, view, self.sems, at, peer)

    def to_core(self):
        view = self.whole.at[self.own]
        return remote(view, view, self.sems, 0, self.peers.core)

    def across(self, cut):
        return self.piece(self.own, self.peers.pair_at, cut, 1 + cut, self.peers.across)

    def to_pair(self, cut):
        return self.piece(self.far, self.peers.pair_at, cut, 1 + GATHER_CUTS + cut, self.peers.pair)

    def far_to_core(self, cut):
        return self.piece(self.far, self.peers.pair_at, cut, 1 + 2 * GATHER_CUTS + cut, self.peers.core)

    def rest_to_core(self, cut):
        return self.piece(self.far, 1 - self.peers.pair_at, cut, 1 + 3 * GATHER_CUTS + cut, self.peers.core)

    def start(self):
        for cut in range(GATHER_CUTS):
            self.across(cut).start()
        self.to_core().start()

    def relay(self, cut):
        self.across(cut).wait_recv()
        self.to_pair(cut).start()
        self.far_to_core(cut).start()

    def relay_rest(self, cut):
        self.to_pair(cut).wait_recv()
        self.rest_to_core(cut).start()

    def wait_near(self):
        self.to_core().wait_recv()

    def wait_far_core(self):
        for cut in range(GATHER_CUTS):
            self.far_to_core(cut).wait_recv()
            self.rest_to_core(cut).wait_recv()

    def drain(self):
        self.to_core().wait_send()
        for cut in range(GATHER_CUTS):
            self.across(cut).wait_send()
            self.to_pair(cut).wait_send()
            self.far_to_core(cut).wait_send()
            self.rest_to_core(cut).wait_send()


GATHER_SEMS = 1 + 4 * GATHER_CUTS


UNIT = 384
PART = UNIT // 2
PIECE = PART // 4
TILE = 48


def add_rows(into, into_at, other, other_at, rows):
    def step(i, carry):
        a = pl.ds(pl.multiple_of(into_at + i * TILE, 16), TILE)
        b = pl.ds(pl.multiple_of(other_at + i * TILE, 16), TILE)
        into[a, :] = (into[a, :].astype(F32) + other[b, :].astype(F32)).astype(BF16)
        return carry

    lax.fori_loop(0, rows // TILE, step, 0)


class Reduce:
    def __init__(self, peers, own, row0, from_core, from_across, from_pair, from_line, from_extra, final, sems):
        self.p = peers
        self.own, self.row0 = own, row0
        self.from_core, self.from_across, self.from_pair = from_core, from_across, from_pair
        self.from_line, self.from_extra, self.final, self.sems = from_line, from_extra, final, sems
        self.core_at = peers.mp % 2
        self.far = flip(peers.mp, 2)

    def view(self, shard, start, rows):
        return self.own.at[shard, pl.ds(pl.multiple_of(self.row0 + start, 16), rows), :]

    def to_core(self, x):
        shard = 2 * x + 1 - self.core_at
        return remote(self.view(shard, 0, UNIT), self.from_core.at[x], self.sems, x, self.p.core)

    def to_across(self):
        return remote(self.view(self.far, 0, UNIT), self.from_across, self.sems, 2, self.p.across)

    def to_pair(self):
        start = (1 - self.p.pair_at) * PART
        return remote(self.view(self.p.mp, start, PART), self.from_pair, self.sems, 3, self.p.pair)

    def to_line(self, step):
        start = self.p.pair_at * PART + self.p.line_slot[step] * PIECE
        return remote(
            self.view(self.p.mp, start, PIECE), self.from_line.at[step], self.sems, 4 + step, self.p.line[step]
        )

    def mine(self):
        return self.p.pair_at * PART + self.p.line_at * PIECE

    def final_view(self, start, rows):
        return self.final.at[pl.ds(pl.multiple_of(self.row0 + start, 16), rows), :]

    def back_line(self, step):
        view = self.final_view(self.mine(), PIECE)
        return remote(view, view, self.sems, 7 + step, self.p.line[step])

    def back_pair(self):
        view = self.final_view(self.p.pair_at * PART, PART)
        return remote(view, view, self.sems, 10, self.p.pair)

    def extra(self, at):
        view = self.final_view(self.mine(), PIECE)
        return remote(view, self.from_extra.at[at], self.sems, 11 + at, self.p.extra[at])

    def start(self):
        for x in range(2):
            self.to_core(x).start()

    def after_core(self):
        for step in range(2):
            x = (self.p.mp // 2 + 1 + step) % 2
            shard = 2 * x + self.core_at
            if step == 0:
                for y in range(2):
                    self.to_core(y).wait_recv()
            add_rows(self.own.at[shard], self.row0, self.from_core.at[x], 0, UNIT)
            if step == 0:
                self.to_across().start()

    def after_across(self):
        self.to_across().wait_recv()
        other = (1 - self.p.pair_at) * PART
        add_rows(self.own.at[self.p.mp], self.row0 + other, self.from_across, other, PART)
        self.to_pair().start()
        mine = self.p.pair_at * PART
        add_rows(self.own.at[self.p.mp], self.row0 + mine, self.from_across, mine, PART)

    def after_pair(self):
        self.to_pair().wait_recv()
        mine = self.p.pair_at * PART
        add_rows(self.own.at[self.p.mp], self.row0 + mine, self.from_pair, 0, PART)
        for step in range(3):
            self.to_line(step).start()

    def after_line(self):
        for step in range(3):
            self.to_line(step).wait_recv()
        at = pl.multiple_of(self.row0 + self.mine(), 16)
        total = self.own[self.p.mp, pl.ds(at, PIECE), :].astype(F32)
        for step in range(3):
            total = total + self.from_line[step].astype(F32)
        self.final[pl.ds(at, PIECE), :] = total.astype(BF16)
        for i in range(len(self.p.extra)):
            self.extra(i).start()
            self.extra(i).wait()
            add_rows(self.final, self.row0 + self.mine(), self.from_extra.at[i], 0, PIECE)
        for step in range(3):
            self.back_line(step).start()

    def after_back_line(self):
        for step in range(3):
            self.back_line(step).wait_recv()
        self.back_pair().start()

    def finish(self):
        self.back_pair().wait_recv()

    def drain(self):
        for x in range(2):
            self.to_core(x).wait_send()
        self.to_across().wait_send()
        self.to_pair().wait_send()
        self.back_pair().wait_send()
        for step in range(3):
            self.to_line(step).wait_send()
            self.back_line(step).wait_send()


REDUCE_SEMS = 11
SMALL = 16


SMALL = 16


class SmallSum:
    def __init__(self, peers, totals, boxes, line_boxes, sems):
        self.p, self.totals, self.boxes, self.line_boxes, self.sems = peers, totals, boxes, line_boxes, sems
        self.pairwise = [peers.core, peers.across, peers.pair]

    def copy(self, at):
        return remote(self.totals.at[at], self.boxes.at[at], self.sems, at, self.pairwise[at])

    def send(self, at):
        self.copy(at).start()

    def add(self, at):
        self.copy(at).wait_recv()
        self.totals[at + 1] = self.totals[at] + self.boxes[at]

    def line_copy(self, step):
        return remote(
            self.totals.at[3], self.line_boxes.at[self.p.line_at], self.sems, 3 + step, self.p.line[step]
        )

    def send_line(self):
        for step in range(3):
            self.line_copy(step).start()
        self.line_boxes[self.p.line_at] = self.totals[3]

    def add_line(self):
        for step in range(3):
            self.line_copy(step).wait_recv()
        self.totals[4] = (self.line_boxes[0] + self.line_boxes[1]) + (self.line_boxes[2] + self.line_boxes[3])
        for at in range(len(self.p.extra)):
            copy = self.extra_copy(at)
            copy.start()
            copy.wait()
            self.totals[5 + at] = self.totals[4 + at] + self.boxes[3 + at]

    def extra_copy(self, at):
        return remote(self.totals.at[4 + at], self.boxes.at[3 + at], self.sems, 6 + at, self.p.extra[at])

    def result(self):
        return self.totals.at[4 + len(self.p.extra)]

    def drain(self):
        for at in range(3):
            self.copy(at).wait_send()
        for step in range(3):
            self.line_copy(step).wait_send()


SMALL_SEMS = 6
SEQ = 256
ROWS = 2 * SEQ
HEADS_HERE = 3
PART_D = D // 4
SCALE = HEAD**-0.5


def dot(left, right, at):
    return lax.dot_general(left, right, ((at[:1], at[1:]), ((), ())), preferred_element_type=F32)


NN, NT, TN = (1, 0), (1, 1), (0, 0)


def mean(v):
    return jnp.sum(v, axis=-1, keepdims=True) * (1.0 / D)


def fold(v):
    return jnp.sum(v.reshape(v.shape[0] // 8, 8, v.shape[1]), axis=0)


def times(count, step):
    def wrapped(i, carry):
        step(i)
        return carry

    lax.fori_loop(0, count, wrapped, 0)


UNITS = 6


def layer_kernel(
    dp_size,
    x_in, c_in, mask, params, bias_in, a_in, u_in, d_in,
    out_hbm, gtok_hbm, ga_hbm, gu_hbm, gd_hbm, small_hbm,
    wa, wu, wd, bias, x, c, qkv, probs, ctx, dctx, y1, r1, mid_low, act, slope, acc, dz, tmp, dlow, out,
    sums, ub_sums, pd, fa, fu, fd,
    from_core, from_across, from_pair, from_line, from_extra,
    small_totals, small_boxes, small_line, sems, small_sems, sa, su, sd, sb, local,
):
    peers = Peers(dp_size)
    diag = {"dp": peers.dp, "mp": flip(flip(peers.mp, 1), 2)}
    me_x, me_c = peers.mp // 2, peers.mp % 2

    def shard(r):
        return 2 * ((me_x + r // 2) % 2) + (me_c + r % 2) % 2

    loads = [
        (a_in, wa.at[peers.mp]),
        (u_in, wu.at[peers.mp]),
        (d_in, wd.at[peers.mp]),
        (bias_in, bias.at[peers.mp]),
        (x_in, x),
        (c_in, c),
    ]
    loads = [pltpu.make_async_copy(src, dst, local.at[i]) for i, (src, dst) in enumerate(loads)]
    for load in (loads[0], loads[3], loads[4], loads[1], loads[2], loads[5]):
        load.start()
    greet([peers.core, peers.across, diag, peers.pair] + peers.line + peers.extra)
    bias_peers = [peers.core, peers.across, diag]
    bias_copies = [
        remote(bias.at[peers.mp], bias.at[peers.mp], sb, i, peer) for i, peer in enumerate(bias_peers)
    ]
    ga_, gu_, gd_ = (Gather(peers, w, s) for w, s in ((wa, sa), (wu, su), (wd, sd)))
    loads[3].wait()
    for copy in bias_copies:
        copy.start()
    for load, g in zip(loads[:3], (ga_, gu_, gd_)):
        load.wait()
        g.start()
    loads[4].wait()
    for copy in bias_copies:
        copy.wait()

    def project(r):
        s = shard(r)
        column = jnp.transpose(bias[s])[0 : 3 * PART_D, 0:1]
        qkv[s] = (dot(wa[s, 0 : 3 * PART_D, :], x[...], NT) + column).astype(BF16)

    def places(s, i):
        head, seq = i // 2, i % 2
        lanes = pl.ds(pl.multiple_of(seq * SEQ, SEQ), SEQ)
        return (
            seq,
            lanes,
            [pl.ds(pl.multiple_of(kind * PART_D + head * HEAD, HEAD), HEAD) for kind in range(3)],
        )

    def attend(r):
        s = shard(r)

        def step(i):
            seq, lanes, (q_at, k_at, v_at) = places(s, i)
            scores = dot(qkv[s, k_at, lanes], qkv[s, q_at, lanes], TN) * SCALE
            keep = mask[pl.ds(pl.multiple_of(seq * SEQ, SEQ), SEQ), :]
            scores = scores * keep + (keep - 1.0) * 1e30
            top = jnp.max(scores, axis=0, keepdims=True)
            weights = jnp.exp(scores - top)
            total = jnp.sum(weights, axis=0, keepdims=True)
            low = (weights * (1.0 / total)).astype(BF16)
            probs[s * 6 + i] = low
            ctx[s, q_at, lanes] = dot(qkv[s, v_at, lanes], low, NN).astype(BF16)

        times(6, step)

    project(0)
    attend(0)
    ga_.relay(0)
    ga_.wait_near()
    project(1)
    ga_.relay(1)
    attend(1)
    ga_.relay_rest(0)
    gu_.relay(0)
    ga_.relay_rest(1)
    gu_.relay(1)
    project(2)
    attend(2)
    ga_.wait_far_core()
    project(3)
    attend(3)
    gu_.relay_rest(0)
    gu_.relay_rest(1)

    wo = wa[:, 3 * PART_D :, :].reshape(D, D)
    acc[...] = dot(ctx[...].reshape(D, ROWS), wo, TN)

    RT = 32

    def rows_of(i, size):
        return pl.ds(pl.multiple_of(i * size, size), size)

    def first_norm(i):
        at = rows_of(i, RT)
        total = x[at, :].astype(F32) + acc[at, :] + params[0:1, :]
        centered = total - mean(total)
        inverse = lax.rsqrt(mean(centered * centered) + EPS)
        scaled = centered * inverse
        y1[at, :] = scaled
        r1[at, :] = jnp.broadcast_to(inverse, (RT, 128))
        mid_low[at, :] = (scaled * params[1:2, :] + params[2:3, :]).astype(BF16)

    times(ROWS // RT, first_norm)

    GT = 16
    gu_.wait_near()

    def feed(r):
        s = shard(r)
        tmp[...] = dot(mid_low[...], wu[s], NN)
        shift = bias[s, 1:2, :]

        def gelu(i):
            at = rows_of(i, GT)
            value = tmp[at, :] + shift
            cdf = 0.5 * (1.0 + lax.erf(value * ROOT_HALF))
            act[s, at, :] = (value * cdf).astype(BF16)
            slope[s, at, :] = (cdf + value * jnp.exp(-0.5 * value * value) * DENSITY).astype(BF16)

        times(ROWS // GT, gelu)

    times(2, feed)
    gd_.relay(0)
    gd_.relay(1)
    gu_.wait_far_core()
    times(2, lambda r: feed(r + 2))
    gd_.relay_rest(0)
    gd_.relay_rest(1)
    gd_.wait_near()
    acc[...] = dot(act[shard(0)], wd[shard(0)], NN)
    acc[...] += dot(act[shard(1)], wd[shard(1)], NN)
    acc[...] += dot(act[shard(2)], wd[shard(2)], NN)
    gd_.wait_far_core()
    acc[...] += dot(act[shard(3)], wd[shard(3)], NN)
    loads[5].wait()
    sums[...] = jnp.zeros_like(sums)
    ub_sums[...] = jnp.zeros_like(ub_sums)

    def second_norm(i):
        at = rows_of(i, RT)
        mid = y1[at, :] * params[1:2, :] + params[2:3, :]
        total = mid + acc[at, :] + params[3:4, :]
        centered = total - mean(total)
        inverse = lax.rsqrt(mean(centered * centered) + EPS)
        scaled = centered * inverse
        gain = params[4:5, :]
        out[at, :] = (scaled * gain + params[5:6, :]).astype(BF16)
        grad = c[at, :].astype(F32)
        weighted = grad * gain
        back = inverse * (weighted - mean(weighted) - scaled * mean(weighted * scaled))
        low = back.astype(BF16)
        dz[at, :] = back
        dlow[at, :] = low
        sums[0] += fold(grad * scaled)
        sums[1] += fold(grad)
        sums[2] += fold(low.astype(F32))

    times(ROWS // RT, second_norm)
    out_copy = pltpu.make_async_copy(out, out_hbm, local.at[6])
    out_copy.start()

    units = []
    for n in range(UNITS):
        own, final = ((pd, fd), (wd, fu), (wu, fa))[n // 2]
        units.append(
            Reduce(
                peers, own, (n % 2) * UNIT, from_core.at[n], from_across.at[n], from_pair.at[n],
                from_line.at[n], from_extra.at[n], final, sems.at[n],
            )
        )

    def down_grads(h):
        def one(r):
            s = shard(r)
            pd[s, h * UNIT : (h + 1) * UNIT, :] = dot(
                dlow[:, h * UNIT : (h + 1) * UNIT], act[s], TN
            ).astype(BF16)

        times(4, one)

    down_grads(0)
    units[0].start()
    down_grads(1)
    units[0].after_core()
    units[1].start()

    def hidden(r):
        s = shard(r)
        tmp[...] = dot(dlow[...], wd[s], NT)

        def scale(i):
            at = rows_of(i, RT)
            low = (tmp[at, :] * slope[s, at, :].astype(F32)).astype(BF16)
            slope[s, at, :] = low
            ub_sums[s] += fold(low.astype(F32))

        times(ROWS // RT, scale)

    times(4, hidden)
    units[1].after_core()
    ga_.drain()
    gu_.drain()
    gd_.drain()

    def up_grads(h):
        def one(r):
            s = shard(r)
            wd[s, h * UNIT : (h + 1) * UNIT, :] = dot(
                mid_low[:, h * UNIT : (h + 1) * UNIT], slope[s], TN
            ).astype(BF16)

        times(4, one)

    up_grads(0)
    units[2].start()
    up_grads(1)
    units[2].after_core()
    units[3].start()
    acc[...] = dot(slope[0], wu[0], NT)
    times(3, lambda r: acc.__setitem__(..., acc[...] + dot(slope[r + 1], wu[r + 1], NT)))
    units[3].after_core()

    def first_norm_back(i):
        at = rows_of(i, RT)
        grad = dz[at, :] + acc[at, :]
        scaled = y1[at, :]
        weighted = grad * params[1:2, :]
        back = r1[at, 0:1] * (weighted - mean(weighted) - scaled * mean(weighted * scaled))
        low = back.astype(BF16)
        dz[at, :] = back
        dlow[at, :] = low
        sums[3] += fold(grad * scaled)
        sums[4] += fold(grad)
        sums[5] += fold(low.astype(F32))

    times(ROWS // RT, first_norm_back)
    units[0].after_across()

    def out_grads(r):
        s = shard(r)
        wu[s, 3 * PART_D :, :] = dot(ctx[s], dlow[...], NN).astype(BF16)
        dctx[s] = dot(wa[s, 3 * PART_D :, :], dlow[...], NT).astype(BF16)

    times(4, out_grads)

    def attend_back(r):
        s = shard(r)

        def step(i):
            seq, lanes, (q_at, k_at, v_at) = places(s, i)
            low = probs[s * 6 + i]
            query, key, value = (qkv[s, at, lanes] for at in (q_at, k_at, v_at))
            grad = dctx[s, q_at, lanes]
            grad_value = dot(grad, low, NT).astype(BF16)
            grad_probs = dot(value, grad, TN)
            wide = low.astype(F32)
            row_total = jnp.sum(wide * grad_probs, axis=0, keepdims=True)
            grad_scores = (wide * (grad_probs - row_total)).astype(BF16)
            qkv[s, q_at, lanes] = (dot(key, grad_scores, NN) * SCALE).astype(BF16)
            qkv[s, k_at, lanes] = (dot(query, grad_scores, NT) * SCALE).astype(BF16)
            qkv[s, v_at, lanes] = grad_value

        times(6, step)

    times(2, attend_back)
    units[0].after_pair()
    units[1].after_across()
    times(2, lambda r: attend_back(r + 2))
    units[0].after_line()
    units[1].after_pair()

    def in_grads(start, rows):
        def one(r):
            s = shard(r)
            wu[s, start : start + rows, :] = dot(qkv[s, start : start + rows, :], x[...], NN).astype(BF16)

        times(4, one)

    in_grads(0, UNIT)
    units[4].start()
    in_grads(UNIT, PART_D)
    units[4].after_core()
    units[5].start()
    small = SmallSum(peers, small_totals, small_boxes, small_line, small_sems)
    ones = jnp.ones((16, ROWS), BF16)

    def pack(r):
        s = shard(r)
        column_sums = dot(ones, qkv[s], NT)
        small_totals[0, pl.ds(s, 1), 0 : 3 * PART_D] = column_sums[0:1, :]
        small_totals[0, pl.ds(s, 1), 3 * PART_D :] = jnp.zeros((1, PART_D), F32)
        small_totals[0, pl.ds(4 + s, 1), :] = jnp.sum(ub_sums[s], axis=0, keepdims=True)

    times(4, pack)
    for i in range(6):
        small_totals[0, 8 + i : 9 + i, :] = jnp.sum(sums[i], axis=0, keepdims=True)
    small_totals[0, 14:16, :] = jnp.zeros((2, D), F32)
    small.send(0)
    units[5].after_core()
    small.add(0)
    small.send(1)

    def token_grads(r):
        s = shard(r)
        dz[...] += dot(qkv[s], wa[s, 0 : 3 * PART_D, :], TN)

    stages = ("after_across", "after_pair", "after_line", "after_back_line", "finish")
    done = [3, 2, 0, 0, 0, 0]
    times(4, token_grads)
    gtok_copy = pltpu.make_async_copy(dz, gtok_hbm, local.at[7])
    gtok_copy.start()
    finals, outs = (fd, fu, fa), (gd_hbm, gu_hbm, ga_hbm)

    def run(n, stage):
        assert done[n] == stage, (n, stage, done)
        done[n] = stage + 1
        getattr(units[n], stages[stage])()
        if n == UNITS - 1:
            if stage == 0:
                small.add(1)
                small.send(2)
            elif stage == 1:
                small.add(2)
                small.send_line()
            elif stage == 2:
                small.add_line()
        if stage == 4 and n % 2 == 1:
            pltpu.make_async_copy(finals[n // 2], outs[n // 2], local.at[8 + n // 2]).start()

    run(2, 0)
    for tick in range(3, UNITS + 4):
        for stage in reversed(range(5)):
            n = tick - stage
            if 0 <= n < UNITS and done[n] == stage:
                run(n, stage)
    for n in range(UNITS):
        while done[n] < 5:
            run(n, done[n])
    small_copy = pltpu.make_async_copy(small.result(), small_hbm, local.at[11])
    small_copy.start()
    for unit in units:
        unit.drain()
    small.drain()
    out_copy.wait()
    gtok_copy.wait()
    for t in range(3):
        pltpu.make_async_copy(finals[t], outs[t], local.at[8 + t]).wait()
    small_copy.wait()


def extras_of(dp_size):
    count, bit = 0, 8
    while bit < dp_size:
        count, bit = count + 1, bit * 2
    return count


def layer(dp_size, x, c, mask, params, bias, a, u, d):
    extras = extras_of(dp_size)
    block = jax.ShapeDtypeStruct((D, D), BF16)
    anywhere = pl.BlockSpec(memory_space=pl.ANY)
    vmem = pl.BlockSpec(memory_space=pltpu.VMEM)
    whole = pltpu.VMEM((4, D, D), BF16)
    low = pltpu.VMEM((ROWS, D), BF16)
    wide = pltpu.VMEM((ROWS, D), F32)
    hidden = pltpu.VMEM((4, ROWS, D), BF16)
    final = pltpu.VMEM((D, D), BF16)
    scratch = dict(
        wa=whole, wu=whole, wd=whole, bias=pltpu.VMEM((4, 8, D), F32), x=low, c=low,
        qkv=pltpu.VMEM((4, 3 * PART_D, ROWS), BF16),
        probs=pltpu.VMEM((24, SEQ, SEQ), BF16),
        ctx=pltpu.VMEM((4, PART_D, ROWS), BF16),
        dctx=pltpu.VMEM((4, PART_D, ROWS), BF16),
        y1=wide, r1=pltpu.VMEM((ROWS, 128), F32), mid_low=low, act=hidden, slope=hidden,
        acc=wide, dz=wide, tmp=wide, dlow=low, out=low,
        sums=pltpu.VMEM((6, 8, D), F32), ub_sums=pltpu.VMEM((4, 8, D), F32), pd=whole,
        fa=final, fu=final, fd=final,
        from_core=pltpu.VMEM((UNITS, 2, UNIT, D), BF16),
        from_across=pltpu.VMEM((UNITS, UNIT, D), BF16),
        from_pair=pltpu.VMEM((UNITS, PART, D), BF16),
        from_line=pltpu.VMEM((UNITS, 3, PIECE, D), BF16),
        from_extra=pltpu.VMEM((UNITS, max(extras, 1), PIECE, D), BF16),
        small_totals=pltpu.VMEM((5 + extras, SMALL, D), F32),
        small_boxes=pltpu.VMEM((3 + extras, SMALL, D), F32),
        small_line=pltpu.VMEM((4, SMALL, D), F32),
        sems=pltpu.SemaphoreType.DMA((UNITS, 2, REDUCE_SEMS + extras)),
        small_sems=pltpu.SemaphoreType.DMA((2, SMALL_SEMS + extras)),
        sa=pltpu.SemaphoreType.DMA((2, GATHER_SEMS)),
        su=pltpu.SemaphoreType.DMA((2, GATHER_SEMS)),
        sd=pltpu.SemaphoreType.DMA((2, GATHER_SEMS)),
        sb=pltpu.SemaphoreType.DMA((2, 3)),
        local=pltpu.SemaphoreType.DMA((12,)),
    )
    return pl.pallas_call(
        functools.partial(layer_kernel, dp_size),
        out_shape=(
            jax.ShapeDtypeStruct((ROWS, D), BF16),
            jax.ShapeDtypeStruct((ROWS, D), F32),
            block,
            block,
            block,
            jax.ShapeDtypeStruct((SMALL, D), F32),
        ),
        in_specs=[anywhere, anywhere, vmem, vmem, anywhere, anywhere, anywhere, anywhere],
        out_specs=(anywhere,) * 6,
        scratch_shapes=list(scratch.values()),
        compiler_params=pltpu.CompilerParams(
            collective_id=0, has_side_effects=True, vmem_limit_bytes=67043328
        ),
    )(x, c, mask, params, bias, a, u, d)


def key_valid(caption_mask, region_counts, group_ids):
    images = region_counts.shape[0]
    match = group_ids[:, None] == jnp.arange(images, dtype=jnp.int32)[None, :]
    regions = jnp.sum(jnp.where(match, region_counts[None, :], 0), axis=1)
    slots = jnp.arange(MAXREG, dtype=jnp.int32)
    return jnp.concatenate([caption_mask > 0, slots[None, :] < regions[:, None]], axis=1)


def body(
    dp_size,
    tokens,
    caption_mask,
    region_counts,
    group_ids,
    query_weight,
    query_bias,
    key_weight,
    value_weight,
    value_bias,
    out_weight,
    out_bias,
    attn_gain,
    attn_shift,
    up_weight,
    up_bias,
    down_weight,
    down_bias,
    final_gain,
    final_shift,
    cotangent,
):
    mp = lax.axis_index("mp")
    seqs = tokens.shape[0] // LEN
    valid = lax.dynamic_slice_in_dim(
        key_valid(caption_mask, region_counts, group_ids), mp * seqs, seqs, 0
    )
    attn_block = jnp.concatenate([query_weight.T, key_weight.T, value_weight.T, out_weight], axis=0)
    part = D // 4
    zeros = jnp.zeros((part,), F32)
    bias = jnp.concatenate(
        [
            jnp.concatenate([query_bias, zeros, value_bias, zeros])[None],
            up_bias[None],
            jnp.zeros((6, D), F32),
        ],
        axis=0,
    )
    params = jnp.stack(
        [out_bias, attn_gain, attn_shift, down_bias, final_gain, final_shift] + [jnp.zeros((D,), F32)] * 2
    )
    fill = ((0, 0), (0, SEQ - LEN), (0, 0))
    spread = lambda v: jnp.pad(v.reshape(seqs, LEN, D), fill).reshape(ROWS, D)
    mask = jnp.pad(valid.astype(F32), fill[:2]).reshape(ROWS, 1)
    out, grad_tokens, ga, gu, gd, small = layer(
        dp_size, spread(tokens), spread(cotangent), mask, params, bias, attn_block, up_weight, down_weight
    )
    trim = lambda v: v.reshape(seqs, SEQ, D)[:, :LEN].reshape(seqs * LEN, D)
    ga = ga.astype(F32)
    mine = lax.dynamic_index_in_dim(small, mp, 0, keepdims=False)
    return (
        trim(out),
        trim(grad_tokens),
        ga[:part].T,
        mine[:part],
        ga[part : 2 * part].T,
        ga[2 * part : 3 * part].T,
        mine[2 * part : 3 * part],
        ga[3 * part :],
        small[13],
        small[11],
        small[12],
        gu.astype(F32),
        lax.dynamic_index_in_dim(small, 4 + mp, 0, keepdims=False),
        gd.astype(F32).T,
        small[10],
        small[8],
        small[9],
    )


def solution(mesh):
    return jax.shard_map(
        functools.partial(body, mesh.shape["dp"]),
        mesh=mesh,
        in_specs=(
            P(("dp", "mp"), None),
            P("dp", None),
            P(),
            P("dp"),
            P(None, "mp"),
            P("mp"),
            P(None, "mp"),
            P(None, "mp"),
            P("mp"),
            P("mp", None),
            P(),
            P(),
            P(),
            P(None, "mp"),
            P("mp"),
            P("mp", None),
            P(),
            P(),
            P(),
            P(("dp", "mp"), None),
        ),
        out_specs=(
            P(("dp", "mp"), None),
            P(("dp", "mp"), None),
            P(None, "mp"),
            P("mp"),
            P(None, "mp"),
            P(None, "mp"),
            P("mp"),
            P("mp", None),
            P(),
            P(),
            P(),
            P(None, "mp"),
            P("mp"),
            P("mp", None),
            P(),
            P(),
            P(),
        ),
        check_vma=False,
    )
```

```python
import functools
import heapq

import jax
import jax.numpy as jnp
from jax import lax
from jax.experimental import pallas as pl
from jax.experimental.pallas import tpu as pltpu
from jax.sharding import PartitionSpec as P

HEAD = 64
MAXREG = 100
EPS = 1e-12
ROOT_HALF = 0.7071067811865476
DENSITY = 0.3989422804014327
MASKED = -1e30

D = 768
LEN = 228
MESH = pl.DeviceIdType.MESH
F32 = jnp.float32
BF16 = jnp.bfloat16


def flip(index, bit):
    return index + bit - 2 * bit * ((index // bit) % 2)


class Peers:
    def __init__(self, dp_size):
        self.dp = lax.axis_index("dp")
        self.mp = lax.axis_index("mp")
        self.core = {"dp": self.dp, "mp": flip(self.mp, 1)}
        self.across = {"dp": self.dp, "mp": flip(self.mp, 2)}
        self.pair_at = self.dp % 2
        self.pair = {"dp": flip(self.dp, 1), "mp": self.mp}
        self.line_at = (self.dp // 2) % 4
        self.next = {"dp": flip(self.dp, 2), "mp": self.mp}
        self.line = []
        self.line_slot = []
        for step in range(1, 4):
            slot = (self.line_at + step) % 4
            self.line_slot.append(slot)
            self.line.append({"dp": self.dp + 2 * (slot - self.line_at), "mp": self.mp})
        self.extra = []
        bit = 8
        while bit < dp_size:
            self.extra.append({"dp": flip(self.dp, bit), "mp": self.mp})
            bit *= 2
        self.cube = [
            self.core,
            self.across,
            self.pair,
            {"dp": flip(self.dp, 2), "mp": self.mp},
            {"dp": flip(self.dp, 4), "mp": self.mp},
        ] + self.extra


def greet(peers):
    barrier = pltpu.get_barrier_semaphore()
    for peer in peers:
        pl.semaphore_signal(barrier, inc=1, device_id=peer, device_id_type=MESH)
    pl.semaphore_wait(barrier, len(peers))


def remote(src, dst, sems, at, peer):
    return pltpu.make_async_remote_copy(
        src_ref=src,
        dst_ref=dst,
        send_sem=sems.at[0, at],
        recv_sem=sems.at[1, at],
        device_id=peer,
        device_id_type=MESH,
    )


QUARTER = D // 4
THIRD = QUARTER // 3


class Gather:
    def __init__(self, peers, whole, sems):
        self.peers, self.whole, self.sems = peers, whole, sems
        self.own = peers.mp
        self.far = flip(peers.mp, 2)

    def piece(self, shard, pair, step, start, rows, at, peer):
        p = (self.peers.pair_at + pair) % 2
        q = (self.peers.line_at + step) % 2
        first = pl.multiple_of((2 * q + p) * QUARTER + start, THIRD)
        view = self.whole.at[shard, pl.ds(first, rows), :]
        return remote(view, view, self.sems, at, peer)

    def to_core(self):
        view = self.whole.at[self.own]
        return remote(view, view, self.sems, 0, self.peers.core)

    def across(self):
        return self.piece(self.own, 0, 0, 0, QUARTER, 1, self.peers.across)

    def across_rest(self):
        return self.piece(self.own, 1, 1, 0, THIRD, 2, self.peers.across)

    def to_pair(self):
        return self.piece(self.far, 0, 0, 0, QUARTER, 3, self.peers.pair)

    def to_next(self):
        return self.piece(self.far, 0, 0, 0, QUARTER, 4, self.peers.next)

    def relay_next(self):
        return self.piece(self.far, 1, 0, THIRD, THIRD, 5, self.peers.next)

    def relay_pair(self):
        return self.piece(self.far, 0, 1, 2 * THIRD, THIRD, 6, self.peers.pair)

    def far_to_core(self, at):
        return self.piece(self.far, at % 2, at // 2, 0, QUARTER, 7 + at, self.peers.core)

    def start(self):
        self.across().start()
        self.across_rest().start()
        self.to_core().start()

    def step1(self):
        self.across().wait_recv()
        self.to_pair().start()
        self.to_next().start()
        self.far_to_core(0).start()

    def step2(self):
        self.to_pair().wait_recv()
        self.relay_next().start()
        self.far_to_core(1).start()
        self.to_next().wait_recv()
        self.relay_pair().start()
        self.far_to_core(2).start()

    def step3(self):
        self.across_rest().wait_recv()
        self.relay_next().wait_recv()
        self.relay_pair().wait_recv()
        self.far_to_core(3).start()

    def wait_near(self):
        self.to_core().wait_recv()

    def wait_far_core(self):
        for at in range(4):
            self.far_to_core(at).wait_recv()

    def drain(self):
        for copy in (
            self.to_core(),
            self.across(),
            self.across_rest(),
            self.to_pair(),
            self.to_next(),
            self.relay_next(),
            self.relay_pair(),
        ):
            copy.wait_send()
        for at in range(4):
            self.far_to_core(at).wait_send()


GATHER_SEMS = 11


DOWN, UP, ATTN = range(3)
ROWS_UNIT = 128
UNITS = tuple((weight, start) for weight in range(3) for start in range(0, D, ROWS_UNIT))


def add_rows(into, into_at, other, other_at, rows):
    tile = next(t for t in (64, 48, 32, 16) if rows % t == 0)

    def step(i, carry):
        a = pl.ds(pl.multiple_of(into_at + i * tile, 16), tile)
        b = pl.ds(pl.multiple_of(other_at + i * tile, 16), tile)
        into[a, :] = (into[a, :].astype(F32) + other[b, :].astype(F32)).astype(BF16)
        return carry

    lax.fori_loop(0, rows // tile, step, 0)


class Reduce:
    def __init__(self, peers, own, row0, rows, from_core, from_across, from_pair, from_line, from_extra, final, sems):
        self.p = peers
        self.own, self.row0, self.rows = own, row0, rows
        self.part, self.piece = rows // 2, rows // 8
        self.from_core, self.from_across, self.from_pair = from_core, from_across, from_pair
        self.from_line, self.from_extra, self.final, self.sems = from_line, from_extra, final, sems
        self.core_at = peers.mp % 2
        self.far = flip(peers.mp, 2)

    def view(self, shard, start, rows):
        return self.own.at[shard, pl.ds(pl.multiple_of(self.row0 + start, 16), rows), :]

    def to_core(self, x):
        shard = 2 * x + 1 - self.core_at
        return remote(self.view(shard, 0, self.rows), self.from_core.at[x], self.sems, x, self.p.core)

    def to_across(self):
        return remote(self.view(self.far, 0, self.rows), self.from_across, self.sems, 2, self.p.across)

    def to_pair(self):
        start = (1 - self.p.pair_at) * self.part
        return remote(self.view(self.p.mp, start, self.part), self.from_pair, self.sems, 3, self.p.pair)

    def to_line(self, step):
        start = self.p.pair_at * self.part + self.p.line_slot[step] * self.piece
        return remote(
            self.view(self.p.mp, start, self.piece), self.from_line.at[step], self.sems, 4 + step, self.p.line[step]
        )

    def mine(self):
        return self.p.pair_at * self.part + self.p.line_at * self.piece

    def final_view(self, start, rows):
        return self.final.at[pl.ds(pl.multiple_of(self.row0 + start, 16), rows), :]

    def back_line(self, step):
        view = self.final_view(self.mine(), self.piece)
        return remote(view, view, self.sems, 7 + step, self.p.line[step])

    def back_pair(self):
        view = self.final_view(self.p.pair_at * self.part, self.part)
        return remote(view, view, self.sems, 10, self.p.pair)

    def extra(self, at):
        view = self.final_view(self.mine(), self.piece)
        return remote(view, self.from_extra.at[at], self.sems, 11 + at, self.p.extra[at])

    def start(self):
        for x in range(2):
            self.to_core(x).start()

    def after_core(self, then):
        for step in range(2):
            x = (self.p.mp // 2 + 1 + step) % 2
            shard = 2 * x + self.core_at
            if step == 0:
                for y in range(2):
                    self.to_core(y).wait_recv()
            add_rows(self.own.at[shard], self.row0, self.from_core.at[x], 0, self.rows)
            if step == 0:
                self.to_across().start()
                then()

    def after_across(self):
        self.to_across().wait_recv()
        other = (1 - self.p.pair_at) * self.part
        add_rows(self.own.at[self.p.mp], self.row0 + other, self.from_across, other, self.part)
        self.to_pair().start()
        mine = self.p.pair_at * self.part
        add_rows(self.own.at[self.p.mp], self.row0 + mine, self.from_across, mine, self.part)

    def after_pair(self):
        self.to_pair().wait_recv()
        mine = self.p.pair_at * self.part
        add_rows(self.own.at[self.p.mp], self.row0 + mine, self.from_pair, 0, self.part)
        for step in range(3):
            self.to_line(step).start()

    def after_line(self):
        for step in range(3):
            self.to_line(step).wait_recv()
        at = pl.multiple_of(self.row0 + self.mine(), 16)
        total = self.own[self.p.mp, pl.ds(at, self.piece), :].astype(F32)
        for step in range(3):
            total = total + self.from_line[step].astype(F32)
        self.final[pl.ds(at, self.piece), :] = total.astype(BF16)
        for i in range(len(self.p.extra)):
            self.extra(i).start()
            self.extra(i).wait()
            add_rows(self.final, self.row0 + self.mine(), self.from_extra.at[i], 0, self.piece)
        for step in range(3):
            self.back_line(step).start()

    def after_back_line(self):
        for step in range(3):
            self.back_line(step).wait_recv()
        self.back_pair().start()

    def finish(self):
        self.back_pair().wait_recv()

    def drain(self):
        for x in range(2):
            self.to_core(x).wait_send()
        self.to_across().wait_send()
        self.to_pair().wait_send()
        self.back_pair().wait_send()
        for step in range(3):
            self.to_line(step).wait_send()
            self.back_line(step).wait_send()


REDUCE_SEMS = 11
SMALL = 16


SMALL = 16


class SmallSum:
    def __init__(self, peers, totals, boxes, line_boxes, sems):
        self.p, self.totals, self.boxes, self.line_boxes, self.sems = peers, totals, boxes, line_boxes, sems
        self.pairwise = [peers.core, peers.across, peers.pair]

    def copy(self, at):
        return remote(self.totals.at[at], self.boxes.at[at], self.sems, at, self.pairwise[at])

    def send(self, at):
        self.copy(at).start()

    def add(self, at):
        self.copy(at).wait_recv()
        self.totals[at + 1] = self.totals[at] + self.boxes[at]

    def line_copy(self, step):
        return remote(
            self.totals.at[3], self.line_boxes.at[self.p.line_at], self.sems, 3 + step, self.p.line[step]
        )

    def send_line(self):
        for step in range(3):
            self.line_copy(step).start()
        self.line_boxes[self.p.line_at] = self.totals[3]

    def add_line(self):
        for step in range(3):
            self.line_copy(step).wait_recv()
        self.totals[4] = (self.line_boxes[0] + self.line_boxes[1]) + (self.line_boxes[2] + self.line_boxes[3])
        for at in range(len(self.p.extra)):
            copy = self.extra_copy(at)
            copy.start()
            copy.wait()
            self.totals[5 + at] = self.totals[4 + at] + self.boxes[3 + at]

    def extra_copy(self, at):
        return remote(self.totals.at[4 + at], self.boxes.at[3 + at], self.sems, 6 + at, self.p.extra[at])

    def result(self):
        return self.totals.at[4 + len(self.p.extra)]

    def drain(self):
        for at in range(3):
            self.copy(at).wait_send()
        for step in range(3):
            self.line_copy(step).wait_send()


SMALL_SEMS = 6
SEQ = 256
ROWS = 2 * SEQ
HEADS_HERE = 3
PART_D = D // 4
SCALE = HEAD**-0.5


def dot(left, right, at):
    return lax.dot_general(left, right, ((at[:1], at[1:]), ((), ())), preferred_element_type=F32)


NN, NT, TN = (1, 0), (1, 1), (0, 0)


def mean(v):
    return jnp.sum(v, axis=-1, keepdims=True) * (1.0 / D)


def fold(v):
    return jnp.sum(v.reshape(v.shape[0] // 8, 8, v.shape[1]), axis=0)


def times(count, step):
    def wrapped(i, carry):
        step(i)
        return carry

    lax.fori_loop(0, count, wrapped, 0)


class Flow:
    UNIT_US = {"core": 1.1, "across": 4.8, "pair": 2.4, "line": 2.4}
    WAY = ("core", "across", "pair", "line", "line", "pair")

    def __init__(self, run):
        self.run = run
        self.now = 0.0
        self.free = dict.fromkeys(self.UNIT_US, 0.0)
        self.events = []

    def send(self, n, stage):
        way = self.WAY[stage]
        self.free[way] = max(self.free[way], self.now) + self.UNIT_US[way]
        heapq.heappush(self.events, (self.free[way] + (1.0 if way == "core" else 3.0), n, stage))

    def one(self):
        at, n, stage = heapq.heappop(self.events)
        self.now = max(self.now, at)
        self.run(n, stage)
        if stage < 5:
            self.send(n, stage + 1)

    def after(self, us):
        self.now += 1.3 * us
        while self.events and self.events[0][0] <= self.now:
            self.one()

    def rest(self):
        while self.events:
            self.one()


def layer_kernel(
    dp_size,
    x_in, c_in, mask, params, bias_in, a_in, u_in, d_in,
    out_hbm, gtok_hbm, ga_hbm, gu_hbm, gd_hbm, small_hbm,
    wa, wu, wd, bias, x, c, qkv, probs, ctx, dctx, y1, r1, mid_low, act, slope, acc, dz, tmp, dlow, out,
    sums, ub_sums, pd, fa, fu, fd,
    from_core, from_across, from_pair, from_line, from_extra,
    small_totals, small_boxes, small_line, sems, small_sems, sa, su, sd, sb, local,
):
    peers = Peers(dp_size)
    diag = {"dp": peers.dp, "mp": flip(flip(peers.mp, 1), 2)}
    me_x, me_c = peers.mp // 2, peers.mp % 2

    def shard(r):
        return 2 * ((me_x + r // 2) % 2) + (me_c + r % 2) % 2

    loads = [
        (a_in, wa.at[peers.mp]),
        (u_in, wu.at[peers.mp]),
        (d_in, wd.at[peers.mp]),
        (bias_in, bias.at[peers.mp]),
        (x_in, x),
        (c_in, c),
    ]
    loads = [pltpu.make_async_copy(src, dst, local.at[i]) for i, (src, dst) in enumerate(loads)]
    for load in (loads[0], loads[3], loads[4], loads[1], loads[2], loads[5]):
        load.start()
    greet([peers.core, peers.across, diag, peers.pair] + peers.line + peers.extra)
    bias_peers = [peers.core, peers.across, diag]
    bias_copies = [
        remote(bias.at[peers.mp], bias.at[peers.mp], sb, i, peer) for i, peer in enumerate(bias_peers)
    ]
    ga_, gu_, gd_ = (Gather(peers, w, s) for w, s in ((wa, sa), (wu, su), (wd, sd)))
    loads[3].wait()
    for copy in bias_copies:
        copy.start()
    for load, g in zip(loads[:3], (ga_, gu_, gd_)):
        load.wait()
        g.start()
    loads[4].wait()
    for copy in bias_copies:
        copy.wait()

    def project(r):
        s = shard(r)
        column = jnp.transpose(bias[s])[0 : 3 * PART_D, 0:1]
        qkv[s] = (dot(wa[s, 0 : 3 * PART_D, :], x[...], NT) + column).astype(BF16)

    def places(s, i):
        head, seq = i // 2, i % 2
        lanes = pl.ds(pl.multiple_of(seq * SEQ, SEQ), SEQ)
        return (
            seq,
            lanes,
            [pl.ds(pl.multiple_of(kind * PART_D + head * HEAD, HEAD), HEAD) for kind in range(3)],
        )

    def attend(r):
        s = shard(r)

        def step(i):
            seq, lanes, (q_at, k_at, v_at) = places(s, i)
            scores = dot(qkv[s, k_at, lanes], qkv[s, q_at, lanes], TN) * SCALE
            keep = mask[pl.ds(pl.multiple_of(seq * SEQ, SEQ), SEQ), :]
            scores = scores * keep + (keep - 1.0) * 1e30
            top = jnp.max(scores, axis=0, keepdims=True)
            weights = jnp.exp(scores - top)
            total = jnp.sum(weights, axis=0, keepdims=True)
            low = (weights * (1.0 / total)).astype(BF16)
            probs[s * 6 + i] = low
            ctx[s, q_at, lanes] = dot(qkv[s, v_at, lanes], low, NN).astype(BF16)

        times(6, step)

    project(0)
    attend(0)
    ga_.step1()
    ga_.wait_near()
    project(1)
    attend(1)
    ga_.step2()
    gu_.step1()
    ga_.step3()
    project(2)
    attend(2)
    ga_.wait_far_core()
    project(3)
    attend(3)
    gu_.step2()
    gd_.step1()

    wo = wa[:, 3 * PART_D :, :].reshape(D, D)
    acc[...] = dot(ctx[...].reshape(D, ROWS), wo, TN)

    RT = 32

    def rows_of(i, size):
        return pl.ds(pl.multiple_of(i * size, size), size)

    def first_norm(i):
        at = rows_of(i, RT)
        total = x[at, :].astype(F32) + acc[at, :] + params[0:1, :]
        centered = total - mean(total)
        inverse = lax.rsqrt(mean(centered * centered) + EPS)
        scaled = centered * inverse
        y1[at, :] = scaled
        r1[at, :] = jnp.broadcast_to(inverse, (RT, 128))
        mid_low[at, :] = (scaled * params[1:2, :] + params[2:3, :]).astype(BF16)

    times(ROWS // RT, first_norm)
    gu_.step3()

    GT = 16
    gu_.wait_near()

    def feed(r):
        s = shard(r)
        tmp[...] = dot(mid_low[...], wu[s], NN)
        shift = bias[s, 1:2, :]

        def gelu(i):
            at = rows_of(i, GT)
            value = tmp[at, :] + shift
            cdf = 0.5 * (1.0 + lax.erf(value * ROOT_HALF))
            act[s, at, :] = (value * cdf).astype(BF16)
            slope[s, at, :] = (cdf + value * jnp.exp(-0.5 * value * value) * DENSITY).astype(BF16)

        times(ROWS // GT, gelu)

    times(2, feed)
    gd_.step2()
    feed(2)
    gd_.step3()
    gu_.wait_far_core()
    feed(3)
    gd_.wait_near()
    acc[...] = dot(act[shard(0)], wd[shard(0)], NN)
    acc[...] += dot(act[shard(1)], wd[shard(1)], NN)
    acc[...] += dot(act[shard(2)], wd[shard(2)], NN)
    gd_.wait_far_core()
    acc[...] += dot(act[shard(3)], wd[shard(3)], NN)
    loads[5].wait()
    sums[...] = jnp.zeros_like(sums)
    ub_sums[...] = jnp.zeros_like(ub_sums)

    def second_norm(i):
        at = rows_of(i, RT)
        mid = y1[at, :] * params[1:2, :] + params[2:3, :]
        total = mid + acc[at, :] + params[3:4, :]
        centered = total - mean(total)
        inverse = lax.rsqrt(mean(centered * centered) + EPS)
        scaled = centered * inverse
        gain = params[4:5, :]
        out[at, :] = (scaled * gain + params[5:6, :]).astype(BF16)
        grad = c[at, :].astype(F32)
        weighted = grad * gain
        back = inverse * (weighted - mean(weighted) - scaled * mean(weighted * scaled))
        low = back.astype(BF16)
        dz[at, :] = back
        dlow[at, :] = low
        sums[0] += fold(grad * scaled)
        sums[1] += fold(grad)
        sums[2] += fold(low.astype(F32))

    times(ROWS // RT, second_norm)
    out_copy = pltpu.make_async_copy(out, out_hbm, local.at[6])
    out_copy.start()

    units = []
    for n, (weight, start) in enumerate(UNITS):
        own, final = ((pd, fd), (wd, fu), (wu, fa))[weight]
        row, rows = n * ROWS_UNIT, ROWS_UNIT
        units.append(
            Reduce(
                peers, own, start, rows,
                from_core.at[:, pl.ds(row, rows), :],
                from_across.at[pl.ds(row, rows), :],
                from_pair.at[pl.ds(row // 2, rows // 2), :],
                from_line.at[:, pl.ds(row // 8, rows // 8), :],
                from_extra.at[:, pl.ds(row // 8, rows // 8), :],
                final, sems.at[n],
            )
        )
    small = SmallSum(peers, small_totals, small_boxes, small_line, small_sems)
    finals, outs = (fd, fu, fa), (gd_hbm, gu_hbm, ga_hbm)
    last = len(UNITS) - 1
    left = [D // ROWS_UNIT] * 3

    def small_after_core():
        small.add(0)
        small.send(1)

    def run(n, stage):
        unit = units[n]
        if stage == 0:
            unit.after_core(small_after_core if n == last else lambda: None)
            return
        (unit.after_across, unit.after_pair, unit.after_line, unit.after_back_line, unit.finish)[stage - 1]()
        if n == last and stage == 1:
            small.add(1)
            small.send(2)
        if n == last and stage == 2:
            small.add(2)
            small.send_line()
        if n == last and stage == 3:
            small.add_line()
        if stage == 5:
            weight = UNITS[n][0]
            left[weight] -= 1
            if left[weight] == 0:
                pltpu.make_async_copy(finals[weight], outs[weight], local.at[8 + weight]).start()

    flow = Flow(run)

    def start(weight, row, rows):
        for n, (other, at) in enumerate(UNITS):
            if other == weight and row <= at < row + rows:
                units[n].start()
                flow.send(n, 0)

    def down_grads(row, rows):
        at = pl.ds(row, rows)

        def one(r):
            s = shard(r)
            pd[s, at, :] = dot(dlow[:, at], act[s], TN).astype(BF16)

        times(4, one)
        start(DOWN, row, rows)

    down_grads(0, 128)
    flow.after(2.0)
    down_grads(128, 256)
    flow.after(2.5)
    down_grads(384, 384)
    flow.after(0.0)

    def hidden(r):
        s = shard(r)
        tmp[...] = dot(dlow[...], wd[s], NT)

        def scale(i):
            at = rows_of(i, RT)
            low = (tmp[at, :] * slope[s, at, :].astype(F32)).astype(BF16)
            slope[s, at, :] = low
            ub_sums[s] += fold(low.astype(F32))

        times(ROWS // RT, scale)

    times(2, hidden)
    flow.after(2.9)
    times(2, lambda r: hidden(r + 2))
    flow.after(2.9)
    ga_.drain()
    gu_.drain()
    gd_.drain()

    def up_grads(row, rows):
        at = pl.ds(row, rows)

        def one(r):
            s = shard(r)
            wd[s, at, :] = dot(mid_low[:, at], slope[s], TN).astype(BF16)

        times(4, one)
        start(UP, row, rows)

    up_grads(0, 384)
    flow.after(2.1)
    up_grads(384, 384)
    flow.after(2.1)
    acc[...] = dot(slope[0], wu[0], NT)
    times(3, lambda r: acc.__setitem__(..., acc[...] + dot(slope[r + 1], wu[r + 1], NT)))
    flow.after(2.9)

    def first_norm_back(i):
        at = rows_of(i, RT)
        grad = dz[at, :] + acc[at, :]
        scaled = y1[at, :]
        weighted = grad * params[1:2, :]
        back = r1[at, 0:1] * (weighted - mean(weighted) - scaled * mean(weighted * scaled))
        low = back.astype(BF16)
        dz[at, :] = back
        dlow[at, :] = low
        sums[3] += fold(grad * scaled)
        sums[4] += fold(grad)
        sums[5] += fold(low.astype(F32))

    times(ROWS // RT, first_norm_back)
    flow.after(2.0)

    def out_grads(r):
        s = shard(r)
        wu[s, 3 * PART_D :, :] = dot(ctx[s], dlow[...], NN).astype(BF16)
        dctx[s] = dot(wa[s, 3 * PART_D :, :], dlow[...], NT).astype(BF16)

    times(4, out_grads)
    flow.after(2.7)

    def attend_back(r):
        s = shard(r)

        def step(i):
            seq, lanes, (q_at, k_at, v_at) = places(s, i)
            low = probs[s * 6 + i]
            query, key, value = (qkv[s, at, lanes] for at in (q_at, k_at, v_at))
            grad = dctx[s, q_at, lanes]
            grad_value = dot(grad, low, NT).astype(BF16)
            grad_probs = dot(value, grad, TN)
            wide = low.astype(F32)
            row_total = jnp.sum(wide * grad_probs, axis=0, keepdims=True)
            grad_scores = (wide * (grad_probs - row_total)).astype(BF16)
            qkv[s, q_at, lanes] = (dot(key, grad_scores, NN) * SCALE).astype(BF16)
            qkv[s, k_at, lanes] = (dot(query, grad_scores, NT) * SCALE).astype(BF16)
            qkv[s, v_at, lanes] = grad_value

        times(6, step)

    for r in range(4):
        attend_back(r)
        flow.after(3.0)

    def in_grads(row, rows):
        def one(r):
            s = shard(r)
            wu[s, row : row + rows, :] = dot(qkv[s, row : row + rows, :], x[...], NN).astype(BF16)

        times(4, one)

    in_grads(0, 2 * PART_D)
    start(ATTN, 0, 2 * PART_D)
    flow.after(2.3)
    in_grads(2 * PART_D, PART_D)
    flow.after(1.2)
    ones = jnp.ones((16, ROWS), BF16)

    def pack(r):
        s = shard(r)
        column_sums = dot(ones, qkv[s], NT)
        small_totals[0, pl.ds(s, 1), 0 : 3 * PART_D] = column_sums[0:1, :]
        small_totals[0, pl.ds(s, 1), 3 * PART_D :] = jnp.zeros((1, PART_D), F32)
        small_totals[0, pl.ds(4 + s, 1), :] = jnp.sum(ub_sums[s], axis=0, keepdims=True)

    times(4, pack)
    for i in range(6):
        small_totals[0, 8 + i : 9 + i, :] = jnp.sum(sums[i], axis=0, keepdims=True)
    small_totals[0, 14:16, :] = jnp.zeros((2, D), F32)
    start(ATTN, 2 * PART_D, 2 * PART_D)
    small.send(0)
    flow.after(1.0)

    def token_grads(r):
        s = shard(r)
        dz[...] += dot(qkv[s], wa[s, 0 : 3 * PART_D, :], TN)

    for r in range(2):
        times(2, lambda i: token_grads(2 * r + i))
        flow.after(2.9)
    gtok_copy = pltpu.make_async_copy(dz, gtok_hbm, local.at[7])
    gtok_copy.start()
    flow.rest()
    small_copy = pltpu.make_async_copy(small.result(), small_hbm, local.at[11])
    small_copy.start()
    for unit in units:
        unit.drain()
    small.drain()
    out_copy.wait()
    gtok_copy.wait()
    for t in range(3):
        pltpu.make_async_copy(finals[t], outs[t], local.at[8 + t]).wait()
    small_copy.wait()


def extras_of(dp_size):
    count, bit = 0, 8
    while bit < dp_size:
        count, bit = count + 1, bit * 2
    return count


def layer(dp_size, x, c, mask, params, bias, a, u, d):
    extras = extras_of(dp_size)
    block = jax.ShapeDtypeStruct((D, D), BF16)
    anywhere = pl.BlockSpec(memory_space=pl.ANY)
    vmem = pl.BlockSpec(memory_space=pltpu.VMEM)
    whole = pltpu.VMEM((4, D, D), BF16)
    low = pltpu.VMEM((ROWS, D), BF16)
    wide = pltpu.VMEM((ROWS, D), F32)
    hidden = pltpu.VMEM((4, ROWS, D), BF16)
    final = pltpu.VMEM((D, D), BF16)
    scratch = dict(
        wa=whole, wu=whole, wd=whole, bias=pltpu.VMEM((4, 8, D), F32), x=low, c=low,
        qkv=pltpu.VMEM((4, 3 * PART_D, ROWS), BF16),
        probs=pltpu.VMEM((24, SEQ, SEQ), BF16),
        ctx=pltpu.VMEM((4, PART_D, ROWS), BF16),
        dctx=pltpu.VMEM((4, PART_D, ROWS), BF16),
        y1=wide, r1=pltpu.VMEM((ROWS, 128), F32), mid_low=low, act=hidden, slope=hidden,
        acc=wide, dz=wide, tmp=wide, dlow=low, out=low,
        sums=pltpu.VMEM((6, 8, D), F32), ub_sums=pltpu.VMEM((4, 8, D), F32), pd=whole,
        fa=final, fu=final, fd=final,
        from_core=pltpu.VMEM((2, 3 * D, D), BF16),
        from_across=pltpu.VMEM((3 * D, D), BF16),
        from_pair=pltpu.VMEM((3 * D // 2, D), BF16),
        from_line=pltpu.VMEM((3, 3 * D // 8, D), BF16),
        from_extra=pltpu.VMEM((max(extras, 1), 3 * D // 8, D), BF16),
        small_totals=pltpu.VMEM((5 + extras, SMALL, D), F32),
        small_boxes=pltpu.VMEM((3 + extras, SMALL, D), F32),
        small_line=pltpu.VMEM((4, SMALL, D), F32),
        sems=pltpu.SemaphoreType.DMA((len(UNITS), 2, REDUCE_SEMS + extras)),
        small_sems=pltpu.SemaphoreType.DMA((2, SMALL_SEMS + extras)),
        sa=pltpu.SemaphoreType.DMA((2, GATHER_SEMS)),
        su=pltpu.SemaphoreType.DMA((2, GATHER_SEMS)),
        sd=pltpu.SemaphoreType.DMA((2, GATHER_SEMS)),
        sb=pltpu.SemaphoreType.DMA((2, 3)),
        local=pltpu.SemaphoreType.DMA((12,)),
    )
    return pl.pallas_call(
        functools.partial(layer_kernel, dp_size),
        out_shape=(
            jax.ShapeDtypeStruct((ROWS, D), BF16),
            jax.ShapeDtypeStruct((ROWS, D), F32),
            block,
            block,
            block,
            jax.ShapeDtypeStruct((SMALL, D), F32),
        ),
        in_specs=[anywhere, anywhere, vmem, vmem, anywhere, anywhere, anywhere, anywhere],
        out_specs=(anywhere,) * 6,
        scratch_shapes=list(scratch.values()),
        compiler_params=pltpu.CompilerParams(
            collective_id=0, has_side_effects=True, vmem_limit_bytes=67043328
        ),
    )(x, c, mask, params, bias, a, u, d)


def key_valid(caption_mask, region_counts, group_ids):
    images = region_counts.shape[0]
    match = group_ids[:, None] == jnp.arange(images, dtype=jnp.int32)[None, :]
    regions = jnp.sum(jnp.where(match, region_counts[None, :], 0), axis=1)
    slots = jnp.arange(MAXREG, dtype=jnp.int32)
    return jnp.concatenate([caption_mask > 0, slots[None, :] < regions[:, None]], axis=1)


def body(
    dp_size,
    tokens,
    caption_mask,
    region_counts,
    group_ids,
    query_weight,
    query_bias,
    key_weight,
    value_weight,
    value_bias,
    out_weight,
    out_bias,
    attn_gain,
    attn_shift,
    up_weight,
    up_bias,
    down_weight,
    down_bias,
    final_gain,
    final_shift,
    cotangent,
):
    mp = lax.axis_index("mp")
    seqs = tokens.shape[0] // LEN
    valid = lax.dynamic_slice_in_dim(
        key_valid(caption_mask, region_counts, group_ids), mp * seqs, seqs, 0
    )
    attn_block = jnp.concatenate([query_weight.T, key_weight.T, value_weight.T, out_weight], axis=0)
    part = D // 4
    zeros = jnp.zeros((part,), F32)
    bias = jnp.concatenate(
        [
            jnp.concatenate([query_bias, zeros, value_bias, zeros])[None],
            up_bias[None],
            jnp.zeros((6, D), F32),
        ],
        axis=0,
    )
    params = jnp.stack(
        [out_bias, attn_gain, attn_shift, down_bias, final_gain, final_shift] + [jnp.zeros((D,), F32)] * 2
    )
    fill = ((0, 0), (0, SEQ - LEN), (0, 0))
    spread = lambda v: jnp.pad(v.reshape(seqs, LEN, D), fill).reshape(ROWS, D)
    mask = jnp.pad(valid.astype(F32), fill[:2]).reshape(ROWS, 1)
    out, grad_tokens, ga, gu, gd, small = layer(
        dp_size, spread(tokens), spread(cotangent), mask, params, bias, attn_block, up_weight, down_weight
    )
    trim = lambda v: v.reshape(seqs, SEQ, D)[:, :LEN].reshape(seqs * LEN, D)
    ga = ga.astype(F32)
    mine = lax.dynamic_index_in_dim(small, mp, 0, keepdims=False)
    return (
        trim(out),
        trim(grad_tokens),
        ga[:part].T,
        mine[:part],
        ga[part : 2 * part].T,
        ga[2 * part : 3 * part].T,
        mine[2 * part : 3 * part],
        ga[3 * part :],
        small[13],
        small[11],
        small[12],
        gu.astype(F32),
        lax.dynamic_index_in_dim(small, 4 + mp, 0, keepdims=False),
        gd.astype(F32).T,
        small[10],
        small[8],
        small[9],
    )


def solution(mesh):
    return jax.shard_map(
        functools.partial(body, mesh.shape["dp"]),
        mesh=mesh,
        in_specs=(
            P(("dp", "mp"), None),
            P("dp", None),
            P(),
            P("dp"),
            P(None, "mp"),
            P("mp"),
            P(None, "mp"),
            P(None, "mp"),
            P("mp"),
            P("mp", None),
            P(),
            P(),
            P(),
            P(None, "mp"),
            P("mp"),
            P("mp", None),
            P(),
            P(),
            P(),
            P(("dp", "mp"), None),
        ),
        out_specs=(
            P(("dp", "mp"), None),
            P(("dp", "mp"), None),
            P(None, "mp"),
            P("mp"),
            P(None, "mp"),
            P(None, "mp"),
            P("mp"),
            P("mp", None),
            P(),
            P(),
            P(),
            P(None, "mp"),
            P("mp"),
            P("mp", None),
            P(),
            P(),
            P(),
        ),
        check_vma=False,
    )
```
